256 devices in a mesh: src: 8 (over y, core), tp: 16 (over x, z_hi), row: 2 (over z_lo).
Axes of the slice: x: 4, y: 4, z: 8 (z_hi: 4, z_lo: 2; z = z_hi * 2 + z_lo), core: 2. Of those that a mesh axis runs over, the one named last changes fastest.
Arguments:
- tokens: bfloat16 [8, 256, 8192], P('src', 'tp', 'row'), may hold values from -6 to 6
- coefficients: float32 [8, 8], replicated, may hold values from -2 to 2
- gate_weights: bfloat16 [8, 8192, 4096], P('src', 'row', 'tp'), may hold values from -0.0625 to 0.0625
- up_weights: bfloat16 [8, 8192, 4096], P('src', 'row', 'tp'), may hold values from -0.0625 to 0.0625
Outputs:
- hidden: bfloat16 [8, 256, 4096], P('src', 'row', 'tp')
The draws below stay inside these ranges and needn't reach their ends.
All inputs are finite; a program needn't handle non-finite values.
Results may differ from the reference program's by a relative error of at most 0.0013.
Values may be sent and summed in bfloat16 or wider, within the bound.
A program may use at most 64 MiB of HBM per device.

```python
import jax
import jax.numpy as jnp
from jax import lax

D = 8192
FF = 4096
TOK = 256
K = 8
M = 8


def block_levels(key, shape, cuts, low, top_value):
    gain, own = 1.0, jax.random.fold_in(key, 6)
    for dim, blocks in cuts:
        steps = jnp.exp(jax.random.uniform(jax.random.fold_in(own, dim), (blocks,), jnp.float32, low / len(cuts), top_value / len(cuts)))
        gain = gain * jnp.repeat(steps, shape[dim] // blocks).reshape([-1 if axis == dim else 1 for axis in range(len(shape))])
    return gain


def noise(key, extent, width, bound, cuts=(), kind=jnp.bfloat16):
    drawn = width * jax.random.normal(key, extent, jnp.float32)
    if cuts:
        drawn = drawn * block_levels(key, extent, cuts, -0.22, 0.18)
    return jnp.clip(drawn, -bound, bound).astype(kind)


def setup_inputs(seed: int = 0) -> dict:
    splits = jax.random.split(jax.random.key(seed), 5)
    tokens = noise(splits[0], (M, TOK, D), 1.0, 6.0, ((0, 8), (1, 16), (2, 2)))
    coefficients = noise(splits[1], (M, K), 0.35, 2.0, (), jnp.float32)
    gate_weights = noise(splits[2], (K, D, FF), D ** -0.5, 0.0625, ((0, 8), (1, 2), (2, 16)))
    up_weights = noise(splits[3], (K, D, FF), D ** -0.5, 0.0625, ((0, 8), (1, 2), (2, 16)))
    return {"tokens": tokens, "coefficients": coefficients, "gate_weights": gate_weights, "up_weights": up_weights}


def reference(tokens, coefficients, gate_weights, up_weights):
    def one_candidate(candidate):
        row_weights = coefficients[candidate]

        def add_source(source, totals):
            merged_gate, merged_up = totals
            gate_slab = lax.dynamic_index_in_dim(gate_weights, source, 0, keepdims=False).astype(jnp.float32)
            up_slab = lax.dynamic_index_in_dim(up_weights, source, 0, keepdims=False).astype(jnp.float32)
            factor = row_weights[source]
            return (merged_gate + factor * gate_slab, merged_up + factor * up_slab)

        zeros_start = jnp.zeros((D, FF), jnp.float32)
        merged_gate, merged_up = lax.fori_loop(0, K, add_source, (zeros_start, zeros_start))
        inputs = tokens[candidate].astype(jnp.float32)
        gate = jnp.dot(inputs, merged_gate, precision=lax.Precision.HIGHEST, preferred_element_type=jnp.float32)
        upper = jnp.dot(inputs, merged_up, precision=lax.Precision.HIGHEST, preferred_element_type=jnp.float32)
        return (jax.nn.silu(gate) * upper).astype(jnp.bfloat16)

    return lax.map(one_candidate, jnp.arange(M))
```

```python
import jax
import jax.numpy as jnp
from jax import lax
from jax.experimental import pallas as pl
from jax.experimental.pallas import tpu as pltpu
from jax.sharding import PartitionSpec as P

MESH = pl.DeviceIdType.MESH
QUARTERS = (0, 3, 1, 2)


def mod4(value):
    return lax.rem(value, jnp.int32(4))


def kernel(
    tok_hbm, coef, gate_hbm, up_hbm, out_ref,
    tok, wts, part, r_sib, z_out, r_z, r_y2, r_y1,
    s_local, s_send, s_z, s_a, s_b, s_b0, s_sib, s_rsib, s_rz, s_ry2, s_ry1,
):
    src, tp, row = lax.axis_index("src"), lax.axis_index("tp"), lax.axis_index("row")
    y, c = lax.div(src, jnp.int32(2)), lax.rem(src, jnp.int32(2))
    x, zh = lax.div(tp, jnp.int32(4)), mod4(tp)
    first = x * (1 - c) + y * c
    last = y * (1 - c) + x * c

    def device(dx=0, dy=0, dz=0):
        return (2 * mod4(y + dy) + c, 4 * mod4(x + dx) + mod4(zh + dz), row)

    def on_a(step):
        return device(dx=step * (1 - c), dy=step * c)

    def on_b(step):
        return device(dx=step * c, dy=step * (1 - c))

    sibling = (2 * y + 1 - c, tp, row)
    partner = (src, tp, 1 - row)

    def slab(q, l, f):
        return ((c * 4 + q) * 4 + l) * 4 + f

    def shards(q, l, f=0, count=1):
        return tok.at[pl.ds(slab(q, l, f), count)]

    def send(ref, there, sem, to, kind=0):
        pltpu.make_async_remote_copy(
            src_ref=ref, dst_ref=there, send_sem=s_send.at[kind], recv_sem=sem, device_id=to, device_id_type=MESH
        ).start()

    def wait(ref, sem):
        pltpu.make_async_copy(ref, ref, sem).wait()

    own = pltpu.make_async_copy(tok_hbm, shards(zh, last, first), s_local.at[0])
    gate_in = pltpu.make_async_copy(gate_hbm.at[0], wts.at[:, pl.ds(0, 256)], s_local.at[1])
    up_in = pltpu.make_async_copy(up_hbm.at[0], wts.at[:, pl.ds(256, 256)], s_local.at[2])
    own.start()
    gate_in.start()
    up_in.start()

    barrier = pltpu.get_barrier_semaphore()
    greeted = [on_a(1), on_a(3), on_b(1), on_b(3), device(dz=1), device(dz=3), device(dz=2), sibling, partner]
    for one in greeted:
        pl.semaphore_signal(barrier, inc=1, device_id=one, device_id_type=MESH)
    own.wait()
    pl.semaphore_wait(barrier, len(greeted))

    qs = [mod4(zh + d) for d in QUARTERS]
    f_minus, f_plus, f_far = mod4(first + 3), mod4(first + 1), mod4(first + 2)
    l_minus, l_plus, l_far = mod4(last + 3), mod4(last + 1), mod4(last + 2)

    def send_a(k):
        one = shards(qs[k], last, first)
        send(one, one, s_a.at[k, 0], on_a(1))
        send(one, one, s_a.at[k, 1], on_a(3))

    def send_b_one(f):
        one = shards(qs[0], last, f)
        send(one, one, s_b.at[0, 0], on_b(1))
        send(one, one, s_b.at[0, 1], on_b(3))

    def send_sib(k, l):
        block = shards(qs[k], l, 0, 4)
        send(block, block, s_sib.at[k], sibling)

    def relay_a(k):
        if k % 2 == 0:
            one = shards(qs[k], last, f_minus)
            send(one, one, s_a.at[k, 2], on_a(1))
        else:
            one = shards(qs[k], last, f_plus)
            send(one, one, s_a.at[k, 2], on_a(3))

    def arrive_a(k):
        wait(shards(qs[k], last, f_minus), s_a.at[k, 0])
        if k % 2 == 0:
            relay_a(k)
        if k == 0:
            send_b_one(f_minus)
        wait(shards(qs[k], last, f_plus), s_a.at[k, 1])
        if k % 2 == 1:
            relay_a(k)
        if k == 0:
            send_b_one(f_plus)

    def finish_a(k):
        wait(shards(qs[k], last, f_far), s_a.at[k, 2])
        if k == 0:
            send_b_one(f_far)
        else:
            block = shards(qs[k], last, 0, 4)
            send(block, block, s_b.at[k, 0], on_b(1))
            send(block, block, s_b.at[k, 1], on_b(3))
        send_sib(k, last)

    def arrive_b(k):
        wait(shards(qs[k], l_minus, 0, 4), s_b.at[k, 0])
        half = shards(qs[k], l_minus, 0, 2)
        send(half, half, s_b.at[k, 2], on_b(1))
        wait(shards(qs[k], l_plus, 0, 4), s_b.at[k, 1])
        half = shards(qs[k], l_plus, 2, 2)
        send(half, half, s_b.at[k, 3], on_b(3))
        send_sib(k, l_minus)
        send_sib(k, l_plus)

    def finish_b(k):
        wait(shards(qs[k], l_far, 0, 2), s_b.at[k, 2])
        wait(shards(qs[k], l_far, 2, 2), s_b.at[k, 3])
        send_sib(k, l_far)

    def part_at(mine, k, i=0, count=4):
        return pl.ds(((0 if mine else 4) + k) * 4 + i, count)

    def multiply(mine, k):
        p = c if mine else 1 - c
        base = (p * 4 + qs[k]) * 16
        rows = [tok[base + i * (4 - 3 * p) + j * (1 + 3 * p)] for i in range(4) for j in range(4)]
        lhs = jnp.concatenate(rows, axis=0)
        for n in range(2):
            prod = jnp.dot(lhs, wts[:, n * 256 : (n + 1) * 256], preferred_element_type=jnp.float32)
            for i in range(4):
                scaled = prod[i * 64 : (i + 1) * 64] * coef[2 * i + p, src]
                part[((0 if mine else 4) + k) * 4 + i, :, :, n * 256 : (n + 1) * 256] = scaled.reshape(4, 16, 256)

    def own_rows(k):
        multiply(True, k)

    def sibling_rows(k):
        wait(tok.at[pl.ds((1 - c) * 64 + qs[k] * 16, 16)], s_sib.at[k])
        multiply(False, k)
        ref = part.at[part_at(False, k)]
        send(ref, r_sib.at[k], s_rsib.at[k], sibling, 1)

    def reduce_a(k):
        wait(r_sib.at[k], s_rsib.at[k])
        away, here = 2 * (1 - row), 2 * row
        at = part_at(True, k)
        z_out[k] = part[at, pl.ds(away, 2)] + r_sib[k, :, pl.ds(away, 2)]
        send(z_out.at[k], r_z.at[k], s_rz.at[k], partner, 1)
        part[at, pl.ds(here, 2)] = part[at, pl.ds(here, 2)] + r_sib[k, :, pl.ds(here, 2)]

    y_minus, y_plus, y_far = mod4(y + 3), mod4(y + 1), mod4(y + 2)

    def reduce_b(k):
        wait(r_z.at[k], s_rz.at[k])
        at = part_at(True, k)
        part[at, pl.ds(2 * row, 2)] = part[at, pl.ds(2 * row, 2)] + r_z[k]
        send(part.at[k * 4 + y_far, 2 * row], r_y2.at[k, 0], s_ry2.at[k, 0], device(dy=1), 1)
        send(part.at[k * 4 + y_far, 2 * row + 1], r_y2.at[k, 1], s_ry2.at[k, 1], device(dy=3), 1)

    def reduce_c(k):
        wait(r_y2.at[k, 0], s_ry2.at[k, 0])
        part[k * 4 + y_plus, 2 * row] = part[k * 4 + y_plus, 2 * row] + r_y2[k, 0]
        send(part.at[k * 4 + y_plus, pl.ds(2 * row, 2)], r_y1.at[k, 0], s_ry1.at[k, 0], device(dy=1), 1)
        wait(r_y2.at[k, 1], s_ry2.at[k, 1])
        part[k * 4 + y_minus, 2 * row + 1] = part[k * 4 + y_minus, 2 * row + 1] + r_y2[k, 1]
        send(part.at[k * 4 + y_minus, pl.ds(2 * row, 2)], r_y1.at[k, 1], s_ry1.at[k, 1], device(dy=3), 1)

    def reduce_d(k):
        wait(r_y1.at[k, 0], s_ry1.at[k, 0])
        wait(r_y1.at[k, 1], s_ry1.at[k, 1])
        for a in range(2):
            total = part[k * 4 + y, 2 * row + a] + r_y1[k, 0, a] + r_y1[k, 1, a]
            gate, up = total[:, :256], total[:, 256:]
            out_ref[a, qs[k]] = (gate / (1.0 + jnp.exp(-gate)) * up).astype(jnp.bfloat16)

    one = shards(zh, last, first)
    send(one, one, s_z.at[0], device(dz=1))
    send(one, one, s_z.at[1], device(dz=3))
    send_a(0)
    send_b_one(first)
    send(one, one, s_z.at[2], device(dz=2))
    arrive_a(0)
    wait(shards(qs[1], last, first), s_z.at[0])
    send_a(1)
    wait(shards(qs[2], last, first), s_z.at[1])
    send_a(2)
    finish_a(0)
    arrive_a(1)
    finish_a(1)
    wait(shards(qs[3], last, first), s_z.at[2])
    send_a(3)
    gate_in.wait()
    up_in.wait()

    arrive_b(0)
    arrive_a(2)
    finish_a(2)
    finish_b(0)
    own_rows(0)
    arrive_b(1)
    arrive_a(3)
    finish_a(3)
    sibling_rows(0)
    finish_b(1)
    own_rows(1)
    reduce_a(0)
    arrive_b(2)
    sibling_rows(1)
    reduce_b(0)
    finish_b(2)
    own_rows(2)
    arrive_b(3)
    reduce_a(1)
    reduce_c(0)
    sibling_rows(2)
    reduce_b(1)
    reduce_d(0)
    finish_b(3)
    own_rows(3)
    reduce_a(2)
    reduce_c(1)
    sibling_rows(3)
    reduce_b(2)
    reduce_d(1)
    reduce_a(3)
    reduce_c(2)
    reduce_b(3)
    reduce_d(2)
    reduce_c(3)
    reduce_d(3)
    wait(tok.at[pl.ds(0, 127)], s_send.at[0])
    wait(part.at[pl.ds(0, 30)], s_send.at[1])


def shards_fn(tokens, coefficients, gate_weights, up_weights):
    dma = pltpu.SemaphoreType.DMA
    hidden = pl.pallas_call(
        kernel,
        out_shape=jax.ShapeDtypeStruct((2, 4, 16, 256), jnp.bfloat16),
        in_specs=[
            pl.BlockSpec(memory_space=pl.ANY),
            pl.BlockSpec(memory_space=pltpu.SMEM),
            pl.BlockSpec(memory_space=pl.ANY),
            pl.BlockSpec(memory_space=pl.ANY),
        ],
        out_specs=pl.BlockSpec(memory_space=pltpu.VMEM),
        scratch_shapes=[
            pltpu.VMEM((128, 16, 4096), jnp.bfloat16),
            pltpu.VMEM((4096, 512), jnp.bfloat16),
            pltpu.VMEM((32, 4, 16, 512), jnp.float32),
            pltpu.VMEM((4, 4, 4, 16, 512), jnp.float32),
            pltpu.VMEM((4, 4, 2, 16, 512), jnp.float32),
            pltpu.VMEM((4, 4, 2, 16, 512), jnp.float32),
            pltpu.VMEM((4, 2, 16, 512), jnp.float32),
            pltpu.VMEM((4, 2, 2, 16, 512), jnp.float32),
            dma((3,)), dma((2,)), dma((3,)), dma((4, 3)), dma((4, 4)), dma((1,)),
            dma((4,)), dma((4,)), dma((4,)), dma((4, 2)), dma((4, 2)),
        ],
        compiler_params=pltpu.CompilerParams(collective_id=0, has_side_effects=True, vmem_limit_bytes=60 * 1024 * 1024),
    )(tokens, coefficients, gate_weights, up_weights)
    return hidden.reshape(1, 128, 256)


def solution(mesh):
    return jax.shard_map(
        shards_fn,
        mesh=mesh,
        in_specs=(P("src", "tp", "row"), P(), P("src", "row", "tp"), P("src", "row", "tp")),
        out_specs=P("src", "row", "tp"),
        check_vma=False,
    )
```

```python
import jax
import jax.numpy as jnp
from jax import lax
from jax.experimental import pallas as pl
from jax.experimental.pallas import tpu as pltpu
from jax.sharding import PartitionSpec as P

MESH = pl.DeviceIdType.MESH


def mod4(value):
    return lax.rem(value, jnp.int32(4))


def kernel(
    tok_hbm, coef, gate_hbm, up_hbm, out_ref,
    tok, wts, part, r_sib, z_out, r_z, r_y,
    s_local, s_send, s_z, s_a, s_b, s_f, s_sib, s_rsib, s_rz, s_ry,
):
    src, tp, row = lax.axis_index("src"), lax.axis_index("tp"), lax.axis_index("row")
    y, c = lax.div(src, jnp.int32(2)), lax.rem(src, jnp.int32(2))
    x, zh = lax.div(tp, jnp.int32(4)), mod4(tp)

    first = x * (1 - c) + y * c

    def last(core):
        return y * (1 - core) + x * core

    def device(dx=0, dy=0, dz=0):
        return (2 * mod4(y + dy) + c, 4 * mod4(x + dx) + mod4(zh + dz), row)

    def on_a(step):
        return device(dx=step * (1 - c), dy=step * c)

    def on_b(step):
        return device(dx=step * c, dy=step * (1 - c))

    sibling = (2 * y + 1 - c, tp, row)
    partner = (src, tp, 1 - row)
    qs = [mod4(zh + d) for d in (0, 3, 1, 2)]
    fs = [mod4(first + d) for d in (0, 3, 1, 2)]

    def shards(k, dl, f=0, count=1):
        return tok.at[pl.ds(((c * 4 + qs[k]) * 4 + mod4(last(c) + dl)) * 4 + f, count)]

    def send(ref, there, sem, to, kind=0):
        pltpu.make_async_remote_copy(
            src_ref=ref, dst_ref=there, send_sem=s_send.at[kind], recv_sem=sem, device_id=to, device_id_type=MESH
        ).start()

    def wait(ref, sem):
        pltpu.make_async_copy(ref, ref, sem).wait()

    own = pltpu.make_async_copy(tok_hbm, shards(0, 0, fs[0]), s_local.at[0])
    gate_in = pltpu.make_async_copy(gate_hbm.at[0], wts.at[:, pl.ds(0, 256)], s_local.at[1])
    up_in = pltpu.make_async_copy(up_hbm.at[0], wts.at[:, pl.ds(256, 256)], s_local.at[2])
    own.start()
    gate_in.start()
    up_in.start()

    barrier = pltpu.get_barrier_semaphore()
    greeted = [device(dx=1), device(dx=3), device(dy=1), device(dy=3), device(dy=2)]
    greeted += [device(dz=1), device(dz=3), device(dz=2), sibling, partner]
    for one in greeted:
        pl.semaphore_signal(barrier, inc=1, device_id=one, device_id_type=MESH)
    own.wait()
    pl.semaphore_wait(barrier, len(greeted))

    def send_b(k, j):
        one = shards(k, 0, fs[j])
        send(one, one, s_b.at[k, 0, j // 2], on_b(1))
        send(one, one, s_b.at[k, 1, j // 2], on_b(3))

    def send_a(k):
        one = shards(k, 0, fs[0])
        send(one, one, s_a.at[k, 0], on_a(1))
        send(one, one, s_a.at[k, 1], on_a(3))

    def relay_a(k):
        one = shards(k, 0, fs[1 + k % 2])
        send(one, one, s_a.at[k, 2], on_a(1 + 2 * (k % 2)))

    def sib(k, dl):
        block = shards(k, dl, 0, 4)
        send(block, block, s_sib.at[k, int(dl == 2)], sibling)

    def start():
        one = shards(0, 0, fs[0])
        send(one, one, s_z.at[0], device(dz=1))
        send(one, one, s_z.at[1], device(dz=3))
        send_a(0)
        send_b(0, 0)
        send(one, one, s_z.at[2], device(dz=2))

    def z(k):
        wait(shards(k, 0, fs[0]), s_z.at[k - 1])
        send_a(k)
        send_b(k, 0)

    def a(k, j):
        wait(shards(k, 0, fs[j]), s_a.at[k, j - 1])
        if j == 1 + k % 2:
            relay_a(k)
        send_b(k, j)
        if j == 3:
            sib(k, 0)

    def b1(k):
        wait(shards(k, 3, 0, 2), s_b.at[k, 0, 0])
        for j in (0, 1):
            one = shards(k, 3, fs[j])
            send(one, one, s_f.at[k, 0], on_b(1))

    def b2(k):
        wait(shards(k, 1, 0, 2), s_b.at[k, 1, 1])
        for j in (2, 3):
            one = shards(k, 1, fs[j])
            send(one, one, s_f.at[k, 1], on_b(3))

    def sib_near(k):
        wait(shards(k, 1, 0, 2), s_b.at[k, 1, 0])
        sib(k, 1)
        wait(shards(k, 3, 0, 2), s_b.at[k, 0, 1])
        sib(k, 3)

    def b3(k):
        wait(shards(k, 2, 0, 2), s_f.at[k, 0])
        wait(shards(k, 2, 0, 2), s_f.at[k, 1])
        sib(k, 2)

    def blocks(portion):
        return (2,) if portion[1] else (0, 1, 3)

    def multiply(mine, portions):
        p = c if mine else 1 - c
        pairs = [(portion[0], mod4(last(p) + d)) for portion in portions for d in blocks(portion)]
        lhs = jnp.concatenate([tok[(p * 4 + qs[k]) * 16 + l * 4 + f] for k, l in pairs for f in range(4)], axis=0)
        for n in range(2):
            prod = jnp.dot(lhs, wts[:, n * 256 : (n + 1) * 256], preferred_element_type=jnp.float32)
            for i, (k, l) in enumerate(pairs):
                for f in range(4):
                    at = (i * 4 + f) * 16
                    scaled = prod[at : at + 16] * coef[2 * (l * (1 - p) + f * p) + p, src]
                    part[((0 if mine else 4) + k) * 4 + l, f, :, n * 256 : (n + 1) * 256] = scaled

    def own_rows(*portions):
        multiply(True, portions)

    def sibling_rows(*portions):
        for portion in portions:
            wait(tok.at[pl.ds(0, 4 * len(blocks(portion)))], s_sib.at[portion])
        multiply(False, portions)
        for portion in portions:
            for d in blocks(portion):
                l = portion[0] * 4 + mod4(last(1 - c) + d)
                send(part.at[16 + l], r_sib.at[l], s_rsib.at[portion], sibling, 1)

    here, away = 2 * row, 2 * (1 - row)

    def reduce_1(k, late):
        wait(r_sib.at[pl.ds(0, len(blocks((k, late))))], s_rsib.at[k, late])

        @pl.when(c == 0)
        def _():
            for d in blocks((k, late)):
                l = k * 4 + mod4(y + d)
                out, there = z_out.at[k, d, pl.ds(0, 2)], r_z.at[k, d, pl.ds(0, 2)]
                out[...] = part[l, pl.ds(away, 2)] + r_sib[l, pl.ds(away, 2)]
                send(out, there, s_rz.at[k, d], partner, 1)
                part[l, pl.ds(here, 2)] = part[l, pl.ds(here, 2)] + r_sib[l, pl.ds(here, 2)]

        @pl.when(c == 1)
        def _():
            for d in blocks((k, late)):
                l = mod4(x + d)

                @pl.when(lax.div(l, jnp.int32(2)) != row)
                def _():
                    z_out[k, d] = part[k * 4 + l] + r_sib[k * 4 + l]
                    send(z_out.at[k, d], r_z.at[k, d], s_rz.at[k, d], partner, 1)

                @pl.when(lax.div(l, jnp.int32(2)) == row)
                def _():
                    part[k * 4 + l] = part[k * 4 + l] + r_sib[k * 4 + l]

    def reduce_2(k, late):
        @pl.when(c == 0)
        def _():
            for d in blocks((k, late)):
                l = k * 4 + mod4(y + d)
                wait(r_z.at[k, d, pl.ds(0, 2)], s_rz.at[k, d])
                part[l, pl.ds(here, 2)] = part[l, pl.ds(here, 2)] + r_z[k, d, pl.ds(0, 2)]
                if d:
                    send(part.at[l, pl.ds(here, 2)], r_y.at[k, d - 1], s_ry.at[k, d - 1, 0], device(dy=d), 1)

        @pl.when(c == 1)
        def _():
            for d in blocks((k, late)):
                l = mod4(x + d)

                @pl.when(lax.div(l, jnp.int32(2)) == row)
                def _():
                    wait(r_z.at[k, d], s_rz.at[k, d])
                    part[k * 4 + l] = part[k * 4 + l] + r_z[k, d]
                    odd = lax.rem(l, jnp.int32(2))
                    for e in (2, 1, 3):
                        spot = part.at[k * 4 + l, mod4(y + e)]
                        send(spot, r_y.at[k, e - 1, odd], s_ry.at[k, e - 1, odd], device(dy=e), 1)

    def finish(k, a, mine):
        total = mine + r_y[k, 0, a] + r_y[k, 1, a] + r_y[k, 2, a]
        gate, up = total[:, :256], total[:, 256:]
        out_ref[a, qs[k]] = (gate / (1.0 + jnp.exp(-gate)) * up).astype(jnp.bfloat16)

    def reduce_3(k):
        @pl.when(c == 0)
        def _():
            for i in (0, 2, 1):
                wait(r_y.at[k, i], s_ry.at[k, i, 0])
            for a in range(2):
                finish(k, a, part[k * 4 + y, here + a])

        @pl.when(c == 1)
        def _():
            for i in (0, 2, 1):
                for a in range(2):
                    wait(r_y.at[k, i, a], s_ry.at[k, i, a])
            for a in range(2):
                finish(k, a, part[k * 4 + here + a, y])

    start()
    a(0,1)
    a(0,2)
    a(0,3)
    z(1)
    z(2)
    b1(0)
    a(1,1)
    a(1,2)
    a(2,1)
    a(2,2)
    b2(0)
    sib_near(0)
    gate_in.wait()
    up_in.wait()
    own_rows((0,0))
    a(1,3)
    z(3)
    a(2,3)
    b1(1)
    sibling_rows((0,0))
    a(3,1)
    a(3,2)
    reduce_1(0,0)
    b2(1)
    a(3,3)
    b3(0)
    sib_near(1)
    own_rows((1,0),(0,1))
    b1(2)
    b2(2)
    b1(3)
    sibling_rows((1,0),(0,1))
    sib_near(2)
    reduce_2(0,0)
    b3(1)
    reduce_1(0,1)
    reduce_1(1,0)
    own_rows((2,0),(1,1))
    b2(3)
    sib_near(3)
    sibling_rows((2,0),(1,1))
    reduce_2(0,1)
    reduce_2(1,0)
    reduce_1(1,1)
    reduce_1(2,0)
    b3(2)
    own_rows((3,0),(2,1))
    sibling_rows((3,0),(2,1))
    reduce_3(0)
    reduce_2(1,1)
    b3(3)
    own_rows((3,1))
    reduce_1(2,1)
    reduce_1(3,0)
    reduce_2(2,0)
    sibling_rows((3,1))
    reduce_3(1)
    reduce_2(2,1)
    reduce_1(3,1)
    reduce_2(3,0)
    reduce_3(2)
    reduce_2(3,1)
    reduce_3(3)
    wait(tok.at[pl.ds(0, 127)], s_send.at[0])
    wait(part.at[pl.ds(0, 30)], s_send.at[1])


def shards_fn(tokens, coefficients, gate_weights, up_weights):
    dma = pltpu.SemaphoreType.DMA
    hidden = pl.pallas_call(
        kernel,
        out_shape=jax.ShapeDtypeStruct((2, 4, 16, 256), jnp.bfloat16),
        in_specs=[
            pl.BlockSpec(memory_space=pl.ANY),
            pl.BlockSpec(memory_space=pltpu.SMEM),
            pl.BlockSpec(memory_space=pl.ANY),
            pl.BlockSpec(memory_space=pl.ANY),
        ],
        out_specs=pl.BlockSpec(memory_space=pltpu.VMEM),
        scratch_shapes=[
            pltpu.VMEM((128, 16, 4096), jnp.bfloat16),
            pltpu.VMEM((4096, 512), jnp.bfloat16),
            pltpu.VMEM((32, 4, 16, 512), jnp.float32),
            pltpu.VMEM((16, 4, 16, 512), jnp.float32),
            pltpu.VMEM((4, 4, 4, 16, 512), jnp.float32),
            pltpu.VMEM((4, 4, 4, 16, 512), jnp.float32),
            pltpu.VMEM((4, 3, 2, 16, 512), jnp.float32),
            dma((3,)), dma((2,)), dma((3,)), dma((4, 3)), dma((4, 2, 2)), dma((4, 2)),
            dma((4, 2)), dma((4, 2)), dma((4, 4)), dma((4, 3, 2)),
        ],
        compiler_params=pltpu.CompilerParams(collective_id=0, has_side_effects=True, vmem_limit_bytes=60 * 1024 * 1024),
    )(tokens, coefficients, gate_weights, up_weights)
    return hidden.reshape(1, 128, 256)


def solution(mesh):
    return jax.shard_map(
        shards_fn,
        mesh=mesh,
        in_specs=(P("src", "tp", "row"), P(), P("src", "row", "tp"), P("src", "row", "tp")),
        out_specs=P("src", "row", "tp"),
        check_vma=False,
    )
```

```python
import jax
import jax.numpy as jnp
from jax import lax
from jax.experimental import pallas as pl
from jax.experimental.pallas import tpu as pltpu
from jax.sharding import PartitionSpec as P

MESH = pl.DeviceIdType.MESH


def mod4(value):
    return lax.rem(value, jnp.int32(4))


def kernel(
    tok_hbm, coef, gate_hbm, up_hbm, out_ref,
    tok, wts, part, r_sib, z_out, r_z, r_y, r_w,
    s_local, s_send, s_z, s_a, s_b, s_f, s_sib, s_rsib, s_rz, s_ry, s_w,
):
    src, tp, row = lax.axis_index("src"), lax.axis_index("tp"), lax.axis_index("row")
    y, c = lax.div(src, jnp.int32(2)), lax.rem(src, jnp.int32(2))
    x, zh = lax.div(tp, jnp.int32(4)), mod4(tp)

    first = x * (1 - c) + y * c

    def last(core):
        return y * (1 - core) + x * core

    def device(dx=0, dy=0, dz=0):
        return (2 * mod4(y + dy) + c, 4 * mod4(x + dx) + mod4(zh + dz), row)

    def on_a(step):
        return device(dx=step * (1 - c), dy=step * c)

    def on_b(step):
        return device(dx=step * c, dy=step * (1 - c))

    sibling = (2 * y + 1 - c, tp, row)
    partner = (src, tp, 1 - row)
    qs = [mod4(zh + d) for d in (0, 3, 1, 2)]
    fs = [mod4(first + d) for d in (0, 3, 1, 2)]

    def shards(k, dl, f=0, count=1):
        return tok.at[pl.ds(((c * 4 + qs[k]) * 4 + mod4(last(c) + dl)) * 4 + f, count)]

    def send(ref, there, sem, to, kind=0):
        pltpu.make_async_remote_copy(
            src_ref=ref, dst_ref=there, send_sem=s_send.at[kind], recv_sem=sem, device_id=to, device_id_type=MESH
        ).start()

    def wait(ref, sem):
        pltpu.make_async_copy(ref, ref, sem).wait()

    own = pltpu.make_async_copy(tok_hbm, shards(0, 0, fs[0]), s_local.at[0])
    gate_in = pltpu.make_async_copy(gate_hbm.at[0], wts.at[:, pl.ds(0, 256)], s_local.at[1])
    up_in = pltpu.make_async_copy(up_hbm.at[0], wts.at[:, pl.ds(256, 256)], s_local.at[2])
    own.start()
    gate_in.start()
    up_in.start()

    barrier = pltpu.get_barrier_semaphore()
    greeted = [device(dx=1), device(dx=3), device(dy=1), device(dy=3), device(dy=2)]
    greeted += [device(dz=1), device(dz=3), device(dz=2), sibling, partner]
    for one in greeted:
        pl.semaphore_signal(barrier, inc=1, device_id=one, device_id_type=MESH)
    own.wait()
    pl.semaphore_wait(barrier, len(greeted))

    def send_b(k, j):
        one = shards(k, 0, fs[j])
        send(one, one, s_b.at[k, 0, j // 2], on_b(1))
        send(one, one, s_b.at[k, 1, j // 2], on_b(3))

    def send_a(k):
        one = shards(k, 0, fs[0])
        send(one, one, s_a.at[k, 0], on_a(1))
        send(one, one, s_a.at[k, 1], on_a(3))

    def relay_a(k):
        one = shards(k, 0, fs[1 + k % 2])
        send(one, one, s_a.at[k, 2], on_a(1 + 2 * (k % 2)))

    def sib(k, dl):
        block = shards(k, dl, 0, 4)
        send(block, block, s_sib.at[k, int(dl == 2)], sibling)

    def send_z(j):
        one = shards(0, 0, fs[j])
        send(one, one, s_z.at[1, j // 2], device(dz=1))
        send(one, one, s_z.at[2, j // 2], device(dz=3))

    def start():
        send_z(0)
        send_a(0)
        send_b(0, 0)

        @pl.when(c == 0)
        def _():
            one = shards(0, 0, fs[0])
            send(one, one, s_z.at[3, 0], device(dz=2))

    def z(k):
        wait(shards(k, 0, fs[0]), s_z.at[k, 0])
        send_a(k)

    def a(k, j):
        wait(shards(k, 0, fs[j]), s_a.at[k, j - 1])
        if j == 1 + k % 2:
            relay_a(k)
        if k == 0:
            send_b(0, j)

            @pl.when(c == 1)
            def _():
                send_z(j)

    def zc(k, half):
        wait(shards(k, 0, 0, 2), s_z.at[k, half])
        if k == half + 1:
            for i in (2 * half, 2 * half + 1):
                one = shards(k, 0, fs[i])
                send(one, one, s_z.at[3, half], device(dz=1 + 2 * half))

    def o(k, half):
        send_b(k, 2 * half)
        send_b(k, 2 * half + 1)

    def b1(k):
        wait(shards(k, 3, 0, 2), s_b.at[k, 0, 0])
        for j in (0, 1):
            one = shards(k, 3, fs[j])
            send(one, one, s_f.at[k, 0], on_b(1))

    def b2(k):
        wait(shards(k, 1, 0, 2), s_b.at[k, 1, 1])
        for j in (2, 3):
            one = shards(k, 1, fs[j])
            send(one, one, s_f.at[k, 1], on_b(3))

    def sib_near(k):
        wait(shards(k, 1, 0, 2), s_b.at[k, 1, 0])
        sib(k, 1)
        wait(shards(k, 3, 0, 2), s_b.at[k, 0, 1])
        sib(k, 3)

    def b3(k):
        wait(shards(k, 2, 0, 2), s_f.at[k, 0])
        wait(shards(k, 2, 0, 2), s_f.at[k, 1])
        sib(k, 2)

    def blocks(portion):
        return (2,) if portion[1] else (0, 1, 3)

    def multiply(mine, portions):
        p = c if mine else 1 - c
        pairs = [(portion[0], mod4(last(p) + d)) for portion in portions for d in blocks(portion)]
        lhs = jnp.concatenate([tok[(p * 4 + qs[k]) * 16 + l * 4 + f] for k, l in pairs for f in range(4)], axis=0)
        for n in range(2):
            prod = jnp.dot(lhs, wts[:, n * 256 : (n + 1) * 256], preferred_element_type=jnp.float32)
            for i, (k, l) in enumerate(pairs):
                for f in range(4):
                    at = (i * 4 + f) * 16
                    scaled = prod[at : at + 16] * coef[2 * (l * (1 - p) + f * p) + p, src]
                    part[((0 if mine else 4) + k) * 4 + l, f, :, n * 256 : (n + 1) * 256] = scaled

    def own_rows(*portions):
        multiply(True, portions)

    def sibling_rows(*portions):
        for portion in portions:
            wait(tok.at[pl.ds(0, 4 * len(blocks(portion)))], s_sib.at[portion])
        multiply(False, portions)
        for portion in portions:
            for d in blocks(portion):
                l = portion[0] * 4 + mod4(last(1 - c) + d)
                send(part.at[16 + l], r_sib.at[l], s_rsib.at[portion], sibling, 1)

    here, away = 2 * row, 2 * (1 - row)

    def reduce_1(k, late):
        wait(r_sib.at[pl.ds(0, len(blocks((k, late))))], s_rsib.at[k, late])

        @pl.when(c == 0)
        def _():
            for d in blocks((k, late)):
                l = k * 4 + mod4(y + d)
                out, there = z_out.at[k, d, pl.ds(0, 2)], r_z.at[k, d, pl.ds(0, 2)]
                out[...] = part[l, pl.ds(away, 2)] + r_sib[l, pl.ds(away, 2)]
                send(out, there, s_rz.at[k, d], partner, 1)
                part[l, pl.ds(here, 2)] = part[l, pl.ds(here, 2)] + r_sib[l, pl.ds(here, 2)]

        @pl.when(c == 1)
        def _():
            for d in blocks((k, late)):
                l = mod4(x + d)

                @pl.when(lax.div(l, jnp.int32(2)) != row)
                def _():
                    z_out[k, d] = part[k * 4 + l] + r_sib[k * 4 + l]
                    send(z_out.at[k, d], r_z.at[k, d], s_rz.at[k, d], partner, 1)

                @pl.when(lax.div(l, jnp.int32(2)) == row)
                def _():
                    part[k * 4 + l] = part[k * 4 + l] + r_sib[k * 4 + l]

    def reduce_2(k, late):
        @pl.when(c == 0)
        def _():
            for d in blocks((k, late)):
                l = k * 4 + mod4(y + d)
                wait(r_z.at[k, d, pl.ds(0, 2)], s_rz.at[k, d])
                part[l, pl.ds(here, 2)] = part[l, pl.ds(here, 2)] + r_z[k, d, pl.ds(0, 2)]
                if d:
                    send(part.at[l, pl.ds(here, 2)], r_y.at[k, d - 1], s_ry.at[k, d - 1, 0], device(dy=d), 1)

        @pl.when(c == 1)
        def _():
            for d in blocks((k, late)):
                l = mod4(x + d)

                @pl.when(lax.div(l, jnp.int32(2)) == row)
                def _():
                    wait(r_z.at[k, d], s_rz.at[k, d])
                    part[k * 4 + l] = part[k * 4 + l] + r_z[k, d]
                    odd = lax.rem(l, jnp.int32(2))
                    for e in (2, 1, 3):
                        spot = part.at[k * 4 + l, mod4(y + e)]
                        send(spot, r_y.at[k, e - 1, odd], s_ry.at[k, e - 1, odd], device(dy=e), 1)

    def activate(k, a, total):
        gate, up = total[:, :256], total[:, 256:]
        out_ref[a, qs[k]] = (gate / (1.0 + jnp.exp(-gate)) * up).astype(jnp.bfloat16)

    def finish(k, a, mine):
        activate(k, a, mine + r_y[k, 0, a] + r_y[k, 1, a] + r_y[k, 2, a])

    def reduce_3(k):
        @pl.when(c == 0)
        def _():
            for i in (0, 2, 1):
                wait(r_y.at[k, i], s_ry.at[k, i, 0])
            for a in range(2):
                finish(k, a, part[k * 4 + y, here + a])

        @pl.when(c == 1)
        def _():
            for i in (0, 2, 1):
                for a in range(2):
                    wait(r_y.at[k, i, a], s_ry.at[k, i, a])
            for a in range(2):
                finish(k, a, part[k * 4 + here + a, y])

    def last_1(late):
        wait(r_sib.at[pl.ds(0, len(blocks((3, late))))], s_rsib.at[3, late])
        for d in blocks((3, late)):
            l = mod4(x + d)
            part[12 + l] = part[12 + l] + r_sib[12 + l]
            for e in (2, 1, 3):
                send(part.at[12 + l, mod4(y + e)], r_w.at[e - 1, l], s_w.at[e - 1, l], device(dy=e), 1)

    def last_2():
        for i in (0, 2, 1):
            for l in range(4):
                wait(r_w.at[i, l], s_w.at[i, l])

        def total(l):
            return part[12 + l, y] + r_w[0, l] + r_w[1, l] + r_w[2, l]

        for i in range(2):
            z_out[3, 0, i] = total(away + i)
        send(z_out.at[3, 0, pl.ds(0, 2)], r_z.at[3, 0, pl.ds(0, 2)], s_rz.at[3, 0], partner, 1)
        for i in range(2):
            z_out[3, 1, i] = total(here + i)

    def last_3():
        wait(r_z.at[3, 0, pl.ds(0, 2)], s_rz.at[3, 0])
        for i in range(2):
            activate(3, i, z_out[3, 1, i] + r_z[3, 0, i])

    start()
    a(0,1)
    a(0,2)
    a(0,3)
    sib(0,0)
    @pl.when(c == 0)
    def _():
        z(1)

    @pl.when(c == 0)
    def _():
        z(2)

    b1(0)
    @pl.when(c == 0)
    def _():
        a(1,1)

    @pl.when(c == 1)
    def _():
        zc(1,0)

    o(1,0)
    @pl.when(c == 0)
    def _():
        a(1,2)

    @pl.when(c == 0)
    def _():
        a(2,1)

    @pl.when(c == 0)
    def _():
        a(2,2)

    @pl.when(c == 1)
    def _():
        zc(2,0)

    b2(0)
    sib_near(0)
    gate_in.wait()
    up_in.wait()
    own_rows((0,0))
    @pl.when(c == 0)
    def _():
        a(1,3)

    @pl.when(c == 1)
    def _():
        zc(1,1)

    o(1,1)
    sib(1,0)
    @pl.when(c == 0)
    def _():
        z(3)

    @pl.when(c == 1)
    def _():
        zc(2,1)

    sibling_rows((0,0))
    b1(1)
    @pl.when(c == 0)
    def _():
        a(2,3)

    o(2,0)
    sib(2,0)
    b3(0)
    @pl.when(c == 0)
    def _():
        a(3,1)

    @pl.when(c == 0)
    def _():
        a(3,2)

    b2(1)
    o(2,1)
    reduce_1(0,0)
    sib_near(1)
    @pl.when(c == 1)
    def _():
        zc(3,0)

    o(3,0)
    own_rows((1,0),(0,1))
    sibling_rows((1,0),(0,1))
    b1(2)
    @pl.when(c == 0)
    def _():
        a(3,3)

    @pl.when(c == 1)
    def _():
        zc(3,1)

    o(3,1)
    sib(3,0)
    reduce_2(0,0)
    reduce_1(0,1)
    reduce_1(1,0)
    b2(2)
    sib_near(2)
    b3(1)
    own_rows((2,0),(1,1))
    b1(3)
    sibling_rows((2,0),(1,1))
    reduce_2(0,1)
    b2(3)
    reduce_2(1,0)
    reduce_1(1,1)
    reduce_1(2,0)
    sib_near(3)
    b3(2)
    own_rows((3,0),(2,1))
    sibling_rows((3,0),(2,1))
    reduce_2(1,1)
    b3(3)
    own_rows((3,1))
    @pl.when(c == 0)
    def _():
        reduce_1(3,0)

    @pl.when(c == 1)
    def _():
        last_1(0)

    reduce_1(2,1)
    reduce_2(2,0)
    sibling_rows((3,1))
    reduce_3(0)
    @pl.when(c == 0)
    def _():
        reduce_1(3,1)

    @pl.when(c == 1)
    def _():
        last_1(1)

    reduce_2(2,1)
    reduce_3(1)
    @pl.when(c == 0)
    def _():
        reduce_2(3,0)

    @pl.when(c == 0)
    def _():
        reduce_2(3,1)

    @pl.when(c == 1)
    def _():
        last_2()

    reduce_3(2)
    @pl.when(c == 0)
    def _():
        reduce_3(3)

    @pl.when(c == 1)
    def _():
        last_3()

    wait(tok.at[pl.ds(0, 127)], s_send.at[0])
    wait(part.at[pl.ds(0, 30)], s_send.at[1])


def shards_fn(tokens, coefficients, gate_weights, up_weights):
    dma = pltpu.SemaphoreType.DMA
    hidden = pl.pallas_call(
        kernel,
        out_shape=jax.ShapeDtypeStruct((2, 4, 16, 256), jnp.bfloat16),
        in_specs=[
            pl.BlockSpec(memory_space=pl.ANY),
            pl.BlockSpec(memory_space=pltpu.SMEM),
            pl.BlockSpec(memory_space=pl.ANY),
            pl.BlockSpec(memory_space=pl.ANY),
        ],
        out_specs=pl.BlockSpec(memory_space=pltpu.VMEM),
        scratch_shapes=[
            pltpu.VMEM((128, 16, 4096), jnp.bfloat16),
            pltpu.VMEM((4096, 512), jnp.bfloat16),
            pltpu.VMEM((32, 4, 16, 512), jnp.float32),
            pltpu.VMEM((16, 4, 16, 512), jnp.float32),
            pltpu.VMEM((4, 4, 4, 16, 512), jnp.float32),
            pltpu.VMEM((4, 4, 4, 16, 512), jnp.float32),
            pltpu.VMEM((4, 3, 2, 16, 512), jnp.float32),
            pltpu.VMEM((3, 4, 16, 512), jnp.float32),
            dma((3,)), dma((2,)), dma((4, 2)), dma((4, 3)), dma((4, 2, 2)), dma((4, 2)),
            dma((4, 2)), dma((4, 2)), dma((4, 4)), dma((4, 3, 2)), dma((3, 4)),
        ],
        compiler_params=pltpu.CompilerParams(collective_id=0, has_side_effects=True, vmem_limit_bytes=60 * 1024 * 1024),
    )(tokens, coefficients, gate_weights, up_weights)
    return hidden.reshape(1, 128, 256)


def solution(mesh):
    return jax.shard_map(
        shards_fn,
        mesh=mesh,
        in_specs=(P("src", "tp", "row"), P(), P("src", "row", "tp"), P("src", "row", "tp")),
        out_specs=P("src", "row", "tp"),
        check_vma=False,
    )
```

```python
import jax
import jax.numpy as jnp
from jax import lax
from jax.experimental import pallas as pl
from jax.experimental.pallas import tpu as pltpu
from jax.sharding import PartitionSpec as P

MESH = pl.DeviceIdType.MESH


def mod4(value):
    return lax.rem(value, jnp.int32(4))


def kernel(
    tok_hbm, coef, gate_hbm, up_hbm, out_ref,
    tok, wts, part, r_sib, z_out, r_z, r_y, r_w,
    s_local, s_send, s_z, s_a, s_b, s_f, s_sib, s_rsib, s_rz, s_ry, s_w,
):
    src, tp, row = lax.axis_index("src"), lax.axis_index("tp"), lax.axis_index("row")
    y, c = lax.div(src, jnp.int32(2)), lax.rem(src, jnp.int32(2))
    x, zh = lax.div(tp, jnp.int32(4)), mod4(tp)

    first = x * (1 - c) + y * c

    def last(core):
        return y * (1 - core) + x * core

    def device(dx=0, dy=0, dz=0):
        return (2 * mod4(y + dy) + c, 4 * mod4(x + dx) + mod4(zh + dz), row)

    def on_a(step):
        return device(dx=step * (1 - c), dy=step * c)

    def on_b(step):
        return device(dx=step * c, dy=step * (1 - c))

    sibling = (2 * y + 1 - c, tp, row)
    partner = (src, tp, 1 - row)
    qs = [mod4(zh + d) for d in (0, 3, 1, 2)]
    fs = [mod4(first + d) for d in (0, 3, 1, 2)]

    def shards(k, dl, f=0, count=1):
        return tok.at[pl.ds(((c * 4 + qs[k]) * 4 + mod4(last(c) + dl)) * 4 + f, count)]

    def send(ref, there, sem, to, kind=0):
        pltpu.make_async_remote_copy(
            src_ref=ref, dst_ref=there, send_sem=s_send.at[kind], recv_sem=sem, device_id=to, device_id_type=MESH
        ).start()

    def wait(ref, sem):
        pltpu.make_async_copy(ref, ref, sem).wait()

    own = pltpu.make_async_copy(tok_hbm, shards(0, 0, fs[0]), s_local.at[0])
    gate_in = pltpu.make_async_copy(gate_hbm.at[0], wts.at[:, pl.ds(0, 256)], s_local.at[1])
    up_in = pltpu.make_async_copy(up_hbm.at[0], wts.at[:, pl.ds(256, 256)], s_local.at[2])
    own.start()
    gate_in.start()
    up_in.start()

    barrier = pltpu.get_barrier_semaphore()
    greeted = [device(dx=1), device(dx=3), device(dy=1), device(dy=3), device(dy=2)]
    greeted += [device(dz=1), device(dz=3), device(dz=2), sibling, partner]
    for one in greeted:
        pl.semaphore_signal(barrier, inc=1, device_id=one, device_id_type=MESH)
    own.wait()
    pl.semaphore_wait(barrier, len(greeted))

    def send_b(k, j):
        one = shards(k, 0, fs[j])
        send(one, one, s_b.at[k, 0, j // 2], on_b(1))
        send(one, one, s_b.at[k, 1, j // 2], on_b(3))

    def send_a(k):
        one = shards(k, 0, fs[0])
        send(one, one, s_a.at[k, 0], on_a(1))
        send(one, one, s_a.at[k, 1], on_a(3))

    def relay_a(k):
        one = shards(k, 0, fs[1 + k % 2])
        send(one, one, s_a.at[k, 2], on_a(1 + 2 * (k % 2)))

    def sib(k, dl):
        block = shards(k, dl, 0, 4)
        send(block, block, s_sib.at[k, int(dl == 2)], sibling)

    def send_z(j):
        one = shards(0, 0, fs[j])
        send(one, one, s_z.at[1, j // 2], device(dz=1))
        send(one, one, s_z.at[2, j // 2], device(dz=3))

    def start():
        send_z(0)
        send_a(0)
        send_b(0, 0)

        @pl.when(c == 0)
        def _():
            one = shards(0, 0, fs[0])
            send(one, one, s_z.at[3, 0], device(dz=2))

    def z(k):
        wait(shards(k, 0, fs[0]), s_z.at[k, 0])
        send_a(k)

    def a(k, j):
        wait(shards(k, 0, fs[j]), s_a.at[k, j - 1])
        if j == 1 + k % 2:
            relay_a(k)
        if k == 0:
            send_b(0, j)

            @pl.when(c == 1)
            def _():
                send_z(j)

    def zc(k, half):
        wait(shards(k, 0, 0, 2), s_z.at[k, half])
        if k == half + 1:
            for i in (2 * half, 2 * half + 1):
                one = shards(k, 0, fs[i])
                send(one, one, s_z.at[3, half], device(dz=1 + 2 * half))

    def o(k, half):
        send_b(k, 2 * half)
        send_b(k, 2 * half + 1)

    def b1(k):
        wait(shards(k, 3, 0, 2), s_b.at[k, 0, 0])
        for j in (0, 1):
            one = shards(k, 3, fs[j])
            send(one, one, s_f.at[k, 0], on_b(1))

    def b2(k):
        wait(shards(k, 1, 0, 2), s_b.at[k, 1, 1])
        for j in (2, 3):
            one = shards(k, 1, fs[j])
            send(one, one, s_f.at[k, 1], on_b(3))

    def sib_near(k):
        wait(shards(k, 1, 0, 2), s_b.at[k, 1, 0])
        sib(k, 1)
        wait(shards(k, 3, 0, 2), s_b.at[k, 0, 1])
        sib(k, 3)

    def b3(k):
        wait(shards(k, 2, 0, 2), s_f.at[k, 0])
        wait(shards(k, 2, 0, 2), s_f.at[k, 1])
        sib(k, 2)

    def blocks(portion):
        return (2,) if portion[1] else (0, 1, 3)

    def multiply(mine, portions):
        p = c if mine else 1 - c
        pairs = [(portion[0], mod4(last(p) + d)) for portion in portions for d in blocks(portion)]
        lhs = jnp.concatenate([tok[(p * 4 + qs[k]) * 16 + l * 4 + f] for k, l in pairs for f in range(4)], axis=0)
        for n in range(2):
            prod = jnp.dot(lhs, wts[:, n * 256 : (n + 1) * 256], preferred_element_type=jnp.float32)
            for i, (k, l) in enumerate(pairs):
                for f in range(4):
                    at = (i * 4 + f) * 16
                    scaled = prod[at : at + 16] * coef[2 * (l * (1 - p) + f * p) + p, src]
                    part[((0 if mine else 4) + k) * 4 + l, f, :, n * 256 : (n + 1) * 256] = scaled

    def own_rows(*portions):
        multiply(True, portions)

    def sibling_rows(*portions):
        for portion in portions:
            wait(tok.at[pl.ds(0, 4 * len(blocks(portion)))], s_sib.at[portion])
        multiply(False, portions)
        for portion in portions:
            for d in blocks(portion):
                l = portion[0] * 4 + mod4(last(1 - c) + d)
                send(part.at[16 + l], r_sib.at[l], s_rsib.at[portion], sibling, 1)

    here, away = 2 * row, 2 * (1 - row)

    def reduce_1(k, late):
        wait(r_sib.at[pl.ds(0, len(blocks((k, late))))], s_rsib.at[k, late])

        @pl.when(c == 0)
        def _():
            for d in blocks((k, late)):
                l = k * 4 + mod4(y + d)
                out, there = z_out.at[k, d, pl.ds(0, 2)], r_z.at[k, d, pl.ds(0, 2)]
                out[...] = part[l, pl.ds(away, 2)] + r_sib[l, pl.ds(away, 2)]
                send(out, there, s_rz.at[k, d], partner, 1)
                part[l, pl.ds(here, 2)] = part[l, pl.ds(here, 2)] + r_sib[l, pl.ds(here, 2)]

        @pl.when(c == 1)
        def _():
            for d in blocks((k, late)):
                l = mod4(x + d)

                @pl.when(lax.div(l, jnp.int32(2)) != row)
                def _():
                    z_out[k, d] = part[k * 4 + l] + r_sib[k * 4 + l]
                    send(z_out.at[k, d], r_z.at[k, d], s_rz.at[k, d], partner, 1)

                @pl.when(lax.div(l, jnp.int32(2)) == row)
                def _():
                    part[k * 4 + l] = part[k * 4 + l] + r_sib[k * 4 + l]

    def reduce_2(k, late):
        @pl.when(c == 0)
        def _():
            for d in blocks((k, late)):
                l = k * 4 + mod4(y + d)
                wait(r_z.at[k, d, pl.ds(0, 2)], s_rz.at[k, d])
                part[l, pl.ds(here, 2)] = part[l, pl.ds(here, 2)] + r_z[k, d, pl.ds(0, 2)]
                if d:
                    send(part.at[l, pl.ds(here, 2)], r_y.at[k, d - 1], s_ry.at[k, d - 1, 0], device(dy=d), 1)

        @pl.when(c == 1)
        def _():
            for d in blocks((k, late)):
                l = mod4(x + d)

                @pl.when(lax.div(l, jnp.int32(2)) == row)
                def _():
                    wait(r_z.at[k, d], s_rz.at[k, d])
                    part[k * 4 + l] = part[k * 4 + l] + r_z[k, d]
                    odd = lax.rem(l, jnp.int32(2))
                    for e in (2, 1, 3):
                        spot = part.at[k * 4 + l, mod4(y + e)]
                        send(spot, r_y.at[k, e - 1, odd], s_ry.at[k, e - 1, odd], device(dy=e), 1)

    def activate(k, a, total):
        gate, up = total[:, :256], total[:, 256:]
        out_ref[a, qs[k]] = (gate / (1.0 + jnp.exp(-gate)) * up).astype(jnp.bfloat16)

    def finish(k, a, mine):
        activate(k, a, mine + r_y[k, 0, a] + r_y[k, 1, a] + r_y[k, 2, a])

    def reduce_3(k):
        @pl.when(c == 0)
        def _():
            for i in (0, 2, 1):
                wait(r_y.at[k, i], s_ry.at[k, i, 0])
            for a in range(2):
                finish(k, a, part[k * 4 + y, here + a])

        @pl.when(c == 1)
        def _():
            for i in (0, 2, 1):
                for a in range(2):
                    wait(r_y.at[k, i, a], s_ry.at[k, i, a])
            for a in range(2):
                finish(k, a, part[k * 4 + here + a, y])

    def last_1(late):
        wait(r_sib.at[pl.ds(0, len(blocks((3, late))))], s_rsib.at[3, late])
        for d in blocks((3, late)):
            l = mod4(x + d)
            part[12 + l] = part[12 + l] + r_sib[12 + l]
            for e in (2, 1, 3):
                send(part.at[12 + l, mod4(y + e)], r_w.at[e - 1, l], s_w.at[e - 1, l], device(dy=e), 1)

    def last_2():
        for i in (0, 2, 1):
            for l in range(4):
                wait(r_w.at[i, l], s_w.at[i, l])

        def total(l):
            return part[12 + l, y] + r_w[0, l] + r_w[1, l] + r_w[2, l]

        for i in range(2):
            z_out[3, 0, i] = total(away + i)
        send(z_out.at[3, 0, pl.ds(0, 2)], r_z.at[3, 0, pl.ds(0, 2)], s_rz.at[3, 0], partner, 1)
        for i in range(2):
            z_out[3, 1, i] = total(here + i)

    def last_3():
        wait(r_z.at[3, 0, pl.ds(0, 2)], s_rz.at[3, 0])
        for i in range(2):
            activate(3, i, z_out[3, 1, i] + r_z[3, 0, i])

    start()
    a(0,1)
    a(0,2)
    a(0,3)
    sib(0,0)
    b1(0)
    @pl.when(c == 0)
    def _():
        z(1)

    @pl.when(c == 0)
    def _():
        z(2)

    b2(0)
    @pl.when(c == 0)
    def _():
        a(1,1)

    @pl.when(c == 1)
    def _():
        zc(1,0)

    o(1,0)
    @pl.when(c == 0)
    def _():
        a(1,2)

    @pl.when(c == 0)
    def _():
        a(2,1)

    @pl.when(c == 0)
    def _():
        a(2,2)

    @pl.when(c == 1)
    def _():
        zc(2,0)

    sib_near(0)
    gate_in.wait()
    up_in.wait()
    own_rows((0,0))
    @pl.when(c == 0)
    def _():
        a(1,3)

    @pl.when(c == 1)
    def _():
        zc(1,1)

    o(1,1)
    sib(1,0)
    @pl.when(c == 0)
    def _():
        z(3)

    @pl.when(c == 1)
    def _():
        zc(2,1)

    sibling_rows((0,0))
    b1(1)
    @pl.when(c == 0)
    def _():
        a(2,3)

    o(2,0)
    sib(2,0)
    b3(0)
    @pl.when(c == 0)
    def _():
        a(3,1)

    @pl.when(c == 0)
    def _():
        a(3,2)

    b2(1)
    o(2,1)
    reduce_1(0,0)
    sib_near(1)
    @pl.when(c == 1)
    def _():
        zc(3,0)

    o(3,0)
    own_rows((1,0),(0,1))
    sibling_rows((1,0),(0,1))
    b1(2)
    @pl.when(c == 0)
    def _():
        a(3,3)

    @pl.when(c == 1)
    def _():
        zc(3,1)

    o(3,1)
    sib(3,0)
    reduce_1(0,1)
    reduce_1(1,0)
    b2(2)
    sib_near(2)
    b3(1)
    own_rows((2,0),(1,1))
    b1(3)
    sibling_rows((2,0),(1,1))
    b2(3)
    reduce_1(1,1)
    reduce_1(2,0)
    sib_near(3)
    reduce_2(0,0)
    reduce_2(0,1)
    reduce_2(1,0)
    b3(2)
    own_rows((3,0),(2,1))
    sibling_rows((3,0),(2,1))
    reduce_2(1,1)
    b3(3)
    own_rows((3,1))
    @pl.when(c == 1)
    def _():
        last_1(0)

    reduce_1(2,1)
    @pl.when(c == 0)
    def _():
        reduce_1(3,0)

    reduce_2(2,0)
    sibling_rows((3,1))
    reduce_3(0)
    @pl.when(c == 0)
    def _():
        reduce_1(3,1)

    @pl.when(c == 1)
    def _():
        last_1(1)

    reduce_2(2,1)
    reduce_3(1)
    @pl.when(c == 0)
    def _():
        reduce_2(3,0)

    @pl.when(c == 0)
    def _():
        reduce_2(3,1)

    @pl.when(c == 1)
    def _():
        last_2()

    reduce_3(2)
    @pl.when(c == 0)
    def _():
        reduce_3(3)

    @pl.when(c == 1)
    def _():
        last_3()

    wait(tok.at[pl.ds(0, 127)], s_send.at[0])
    wait(part.at[pl.ds(0, 30)], s_send.at[1])


def shards_fn(tokens, coefficients, gate_weights, up_weights):
    dma = pltpu.SemaphoreType.DMA
    hidden = pl.pallas_call(
        kernel,
        out_shape=jax.ShapeDtypeStruct((2, 4, 16, 256), jnp.bfloat16),
        in_specs=[
            pl.BlockSpec(memory_space=pl.ANY),
            pl.BlockSpec(memory_space=pltpu.SMEM),
            pl.BlockSpec(memory_space=pl.ANY),
            pl.BlockSpec(memory_space=pl.ANY),
        ],
        out_specs=pl.BlockSpec(memory_space=pltpu.VMEM),
        scratch_shapes=[
            pltpu.VMEM((128, 16, 4096), jnp.bfloat16),
            pltpu.VMEM((4096, 512), jnp.bfloat16),
            pltpu.VMEM((32, 4, 16, 512), jnp.float32),
            pltpu.VMEM((16, 4, 16, 512), jnp.float32),
            pltpu.VMEM((4, 4, 4, 16, 512), jnp.float32),
            pltpu.VMEM((4, 4, 4, 16, 512), jnp.float32),
            pltpu.VMEM((4, 3, 2, 16, 512), jnp.float32),
            pltpu.VMEM((3, 4, 16, 512), jnp.float32),
            dma((3,)), dma((2,)), dma((4, 2)), dma((4, 3)), dma((4, 2, 2)), dma((4, 2)),
            dma((4, 2)), dma((4, 2)), dma((4, 4)), dma((4, 3, 2)), dma((3, 4)),
        ],
        compiler_params=pltpu.CompilerParams(collective_id=0, has_side_effects=True, vmem_limit_bytes=60 * 1024 * 1024),
    )(tokens, coefficients, gate_weights, up_weights)
    return hidden.reshape(1, 128, 256)


def solution(mesh):
    return jax.shard_map(
        shards_fn,
        mesh=mesh,
        in_specs=(P("src", "tp", "row"), P(), P("src", "row", "tp"), P("src", "row", "tp")),
        out_specs=P("src", "row", "tp"),
        check_vma=False,
    )
```

```python
import jax
import jax.numpy as jnp
from jax import lax
from jax.experimental import pallas as pl
from jax.experimental.pallas import tpu as pltpu
from jax.sharding import PartitionSpec as P

MESH = pl.DeviceIdType.MESH


def mod4(value):
    return lax.rem(value, jnp.int32(4))


def kernel(
    tok_hbm, coef, gate_hbm, up_hbm, out_ref,
    tok, wts, part, r_sib, z_out, r_z, r_y, r_w,
    s_local, s_send, s_z, s_a, s_b, s_f, s_sib, s_rsib, s_rz, s_ry, s_w,
):
    src, tp, row = lax.axis_index("src"), lax.axis_index("tp"), lax.axis_index("row")
    y, c = lax.div(src, jnp.int32(2)), lax.rem(src, jnp.int32(2))
    x, zh = lax.div(tp, jnp.int32(4)), mod4(tp)

    first = x * (1 - c) + y * c

    def last(core):
        return y * (1 - core) + x * core

    def device(dx=0, dy=0, dz=0):
        return (2 * mod4(y + dy) + c, 4 * mod4(x + dx) + mod4(zh + dz), row)

    def on_a(step):
        return device(dx=step * (1 - c), dy=step * c)

    def on_b(step):
        return device(dx=step * c, dy=step * (1 - c))

    sibling = (2 * y + 1 - c, tp, row)
    partner = (src, tp, 1 - row)
    qs = [mod4(zh + d) for d in (0, 3, 1, 2)]
    fs = [mod4(first + d) for d in (0, 3, 1, 2)]

    def shards(k, dl, f=0, count=1):
        return tok.at[pl.ds(((c * 4 + qs[k]) * 4 + mod4(last(c) + dl)) * 4 + f, count)]

    def send(ref, there, sem, to, kind=0):
        pltpu.make_async_remote_copy(
            src_ref=ref, dst_ref=there, send_sem=s_send.at[kind], recv_sem=sem, device_id=to, device_id_type=MESH
        ).start()

    def wait(ref, sem):
        pltpu.make_async_copy(ref, ref, sem).wait()

    own = pltpu.make_async_copy(tok_hbm, shards(0, 0, fs[0]), s_local.at[0])
    gate_in = pltpu.make_async_copy(gate_hbm.at[0], wts.at[:, pl.ds(0, 256)], s_local.at[1])
    up_in = pltpu.make_async_copy(up_hbm.at[0], wts.at[:, pl.ds(256, 256)], s_local.at[2])
    own.start()
    gate_in.start()
    up_in.start()

    barrier = pltpu.get_barrier_semaphore()
    greeted = [device(dx=1), device(dx=3), device(dx=2), device(dy=1), device(dy=3), device(dy=2)]
    greeted += [device(dz=1), device(dz=3), device(dz=2), sibling, partner]
    for one in greeted:
        pl.semaphore_signal(barrier, inc=1, device_id=one, device_id_type=MESH)
    own.wait()
    pl.semaphore_wait(barrier, len(greeted))

    def send_b(k, j):
        one = shards(k, 0, fs[j])
        send(one, one, s_b.at[k, 0, j // 2], on_b(1))
        send(one, one, s_b.at[k, 1, j // 2], on_b(3))

    def send_a(k):
        one = shards(k, 0, fs[0])
        send(one, one, s_a.at[k, 0], on_a(1))
        send(one, one, s_a.at[k, 1], on_a(3))
        if k == 0:
            send(one, one, s_a.at[k, 2], on_a(2))

    def relay_a(k):
        one = shards(k, 0, fs[1 + k % 2])
        send(one, one, s_a.at[k, 2], on_a(1 + 2 * (k % 2)))

    def sib(k, dl):
        block = shards(k, dl, 0, 4)
        send(block, block, s_sib.at[k, int(dl == 2)], sibling)

    def send_z(j):
        one = shards(0, 0, fs[j])
        send(one, one, s_z.at[1, j // 2], device(dz=1))
        send(one, one, s_z.at[2, j // 2], device(dz=3))

    def start():
        send_z(0)
        send_a(0)
        send_b(0, 0)

        @pl.when(c == 0)
        def _():
            one = shards(0, 0, fs[0])
            send(one, one, s_z.at[3, 0], device(dz=2))

    def z(k):
        wait(shards(k, 0, fs[0]), s_z.at[k, 0])
        send_a(k)

    def a(k, j):
        wait(shards(k, 0, fs[j]), s_a.at[k, j - 1])
        if k > 0 and j == 1 + k % 2:
            relay_a(k)
        if k == 0:
            send_b(0, j)

            @pl.when(c == 1)
            def _():
                send_z(j)

    def zc(k, half):
        wait(shards(k, 0, 0, 2), s_z.at[k, half])
        if k == half + 1:
            for i in (2 * half, 2 * half + 1):
                one = shards(k, 0, fs[i])
                send(one, one, s_z.at[3, half], device(dz=1 + 2 * half))

    def o(k, half):
        send_b(k, 2 * half)
        send_b(k, 2 * half + 1)

    def b1(k):
        wait(shards(k, 3, 0, 2), s_b.at[k, 0, 0])
        for j in (0, 1):
            one = shards(k, 3, fs[j])
            send(one, one, s_f.at[k, 0], on_b(1))

    def b2(k):
        wait(shards(k, 1, 0, 2), s_b.at[k, 1, 1])
        for j in (2, 3):
            one = shards(k, 1, fs[j])
            send(one, one, s_f.at[k, 1], on_b(3))

    def sib_near(k):
        wait(shards(k, 1, 0, 2), s_b.at[k, 1, 0])
        sib(k, 1)
        wait(shards(k, 3, 0, 2), s_b.at[k, 0, 1])
        sib(k, 3)

    def b3(k):
        wait(shards(k, 2, 0, 2), s_f.at[k, 0])
        wait(shards(k, 2, 0, 2), s_f.at[k, 1])
        sib(k, 2)

    def blocks(portion):
        return (2,) if portion[1] else (0, 1, 3)

    def multiply(mine, portions):
        p = c if mine else 1 - c
        pairs = [(portion[0], mod4(last(p) + d)) for portion in portions for d in blocks(portion)]
        lhs = jnp.concatenate([tok[(p * 4 + qs[k]) * 16 + l * 4 + f] for k, l in pairs for f in range(4)], axis=0)
        for n in range(2):
            prod = jnp.dot(lhs, wts[:, n * 256 : (n + 1) * 256], preferred_element_type=jnp.float32)
            for i, (k, l) in enumerate(pairs):
                for f in range(4):
                    at = (i * 4 + f) * 16
                    scaled = prod[at : at + 16] * coef[2 * (l * (1 - p) + f * p) + p, src]
                    part[((0 if mine else 4) + k) * 4 + l, f, :, n * 256 : (n + 1) * 256] = scaled

    def own_rows(*portions):
        multiply(True, portions)

    def sibling_rows(*portions):
        for portion in portions:
            wait(tok.at[pl.ds(0, 4 * len(blocks(portion)))], s_sib.at[portion])
        multiply(False, portions)
        for portion in portions:
            for d in blocks(portion):
                l = portion[0] * 4 + mod4(last(1 - c) + d)
                send(part.at[16 + l], r_sib.at[l], s_rsib.at[portion], sibling, 1)

    here, away = 2 * row, 2 * (1 - row)

    def reduce_1(k, late):
        wait(r_sib.at[pl.ds(0, len(blocks((k, late))))], s_rsib.at[k, late])

        @pl.when(c == 0)
        def _():
            for d in blocks((k, late)):
                l = k * 4 + mod4(y + d)
                out, there = z_out.at[k, d, pl.ds(0, 2)], r_z.at[k, d, pl.ds(0, 2)]
                out[...] = part[l, pl.ds(away, 2)] + r_sib[l, pl.ds(away, 2)]
                send(out, there, s_rz.at[k, d], partner, 1)
                part[l, pl.ds(here, 2)] = part[l, pl.ds(here, 2)] + r_sib[l, pl.ds(here, 2)]

        @pl.when(c == 1)
        def _():
            for d in blocks((k, late)):
                l = mod4(x + d)

                @pl.when(lax.div(l, jnp.int32(2)) != row)
                def _():
                    z_out[k, d] = part[k * 4 + l] + r_sib[k * 4 + l]
                    send(z_out.at[k, d], r_z.at[k, d], s_rz.at[k, d], partner, 1)

                @pl.when(lax.div(l, jnp.int32(2)) == row)
                def _():
                    part[k * 4 + l] = part[k * 4 + l] + r_sib[k * 4 + l]

    def reduce_2(k, late):
        @pl.when(c == 0)
        def _():
            for d in blocks((k, late)):
                l = k * 4 + mod4(y + d)
                wait(r_z.at[k, d, pl.ds(0, 2)], s_rz.at[k, d])
                part[l, pl.ds(here, 2)] = part[l, pl.ds(here, 2)] + r_z[k, d, pl.ds(0, 2)]
                if d:
                    send(part.at[l, pl.ds(here, 2)], r_y.at[k, d - 1], s_ry.at[k, d - 1, 0], device(dy=d), 1)

        @pl.when(c == 1)
        def _():
            for d in blocks((k, late)):
                l = mod4(x + d)

                @pl.when(lax.div(l, jnp.int32(2)) == row)
                def _():
                    wait(r_z.at[k, d], s_rz.at[k, d])
                    part[k * 4 + l] = part[k * 4 + l] + r_z[k, d]
                    odd = lax.rem(l, jnp.int32(2))
                    for e in (2, 1, 3):
                        spot = part.at[k * 4 + l, mod4(y + e)]
                        send(spot, r_y.at[k, e - 1, odd], s_ry.at[k, e - 1, odd], device(dy=e), 1)

    def activate(k, a, total):
        gate, up = total[:, :256], total[:, 256:]
        out_ref[a, qs[k]] = (gate / (1.0 + jnp.exp(-gate)) * up).astype(jnp.bfloat16)

    def finish(k, a, mine):
        activate(k, a, mine + r_y[k, 0, a] + r_y[k, 1, a] + r_y[k, 2, a])

    def reduce_3(k):
        @pl.when(c == 0)
        def _():
            for i in (0, 2, 1):
                wait(r_y.at[k, i], s_ry.at[k, i, 0])
            for a in range(2):
                finish(k, a, part[k * 4 + y, here + a])

        @pl.when(c == 1)
        def _():
            for i in (0, 2, 1):
                for a in range(2):
                    wait(r_y.at[k, i, a], s_ry.at[k, i, a])
            for a in range(2):
                finish(k, a, part[k * 4 + here + a, y])

    def last_1(late):
        wait(r_sib.at[pl.ds(0, len(blocks((3, late))))], s_rsib.at[3, late])
        for d in blocks((3, late)):
            l = mod4(x + d)
            part[12 + l] = part[12 + l] + r_sib[12 + l]
            for e in (2, 1, 3):
                send(part.at[12 + l, mod4(y + e)], r_w.at[e - 1, l], s_w.at[e - 1, l], device(dy=e), 1)

    def last_2():
        for i in (0, 2, 1):
            for l in range(4):
                wait(r_w.at[i, l], s_w.at[i, l])

        def total(l):
            return part[12 + l, y] + r_w[0, l] + r_w[1, l] + r_w[2, l]

        for i in range(2):
            z_out[3, 0, i] = total(away + i)
        send(z_out.at[3, 0, pl.ds(0, 2)], r_z.at[3, 0, pl.ds(0, 2)], s_rz.at[3, 0], partner, 1)
        for i in range(2):
            z_out[3, 1, i] = total(here + i)

    def last_3():
        wait(r_z.at[3, 0, pl.ds(0, 2)], s_rz.at[3, 0])
        for i in range(2):
            activate(3, i, z_out[3, 1, i] + r_z[3, 0, i])

    start()
    a(0,1)
    a(0,2)
    a(0,3)
    sib(0,0)
    b1(0)
    @pl.when(c == 0)
    def _():
        z(1)

    @pl.when(c == 0)
    def _():
        z(2)

    b2(0)
    @pl.when(c == 0)
    def _():
        a(1,1)

    @pl.when(c == 1)
    def _():
        zc(1,0)

    o(1,0)
    @pl.when(c == 0)
    def _():
        a(1,2)

    @pl.when(c == 0)
    def _():
        a(2,1)

    @pl.when(c == 0)
    def _():
        a(2,2)

    @pl.when(c == 1)
    def _():
        zc(2,0)

    sib_near(0)
    gate_in.wait()
    up_in.wait()
    own_rows((0,0))
    @pl.when(c == 0)
    def _():
        a(1,3)

    @pl.when(c == 1)
    def _():
        zc(1,1)

    o(1,1)
    sib(1,0)
    @pl.when(c == 0)
    def _():
        z(3)

    @pl.when(c == 1)
    def _():
        zc(2,1)

    sibling_rows((0,0))
    b1(1)
    @pl.when(c == 0)
    def _():
        a(2,3)

    o(2,0)
    sib(2,0)
    b3(0)
    @pl.when(c == 0)
    def _():
        a(3,1)

    @pl.when(c == 0)
    def _():
        a(3,2)

    b2(1)
    o(2,1)
    reduce_1(0,0)
    sib_near(1)
    @pl.when(c == 1)
    def _():
        zc(3,0)

    o(3,0)
    own_rows((1,0),(0,1))
    sibling_rows((1,0),(0,1))
    b1(2)
    @pl.when(c == 0)
    def _():
        a(3,3)

    @pl.when(c == 1)
    def _():
        zc(3,1)

    o(3,1)
    sib(3,0)
    reduce_1(0,1)
    reduce_1(1,0)
    b2(2)
    sib_near(2)
    b3(1)
    own_rows((2,0),(1,1))
    b1(3)
    sibling_rows((2,0),(1,1))
    b2(3)
    reduce_1(1,1)
    reduce_1(2,0)
    sib_near(3)
    reduce_2(0,0)
    reduce_2(0,1)
    reduce_2(1,0)
    b3(2)
    own_rows((3,0),(2,1))
    sibling_rows((3,0),(2,1))
    reduce_2(1,1)
    b3(3)
    own_rows((3,1))
    @pl.when(c == 1)
    def _():
        last_1(0)

    reduce_1(2,1)
    @pl.when(c == 0)
    def _():
        reduce_1(3,0)

    reduce_2(2,0)
    sibling_rows((3,1))
    reduce_3(0)
    @pl.when(c == 0)
    def _():
        reduce_1(3,1)

    @pl.when(c == 1)
    def _():
        last_1(1)

    reduce_2(2,1)
    reduce_3(1)
    @pl.when(c == 0)
    def _():
        reduce_2(3,0)

    @pl.when(c == 0)
    def _():
        reduce_2(3,1)

    @pl.when(c == 1)
    def _():
        last_2()

    reduce_3(2)
    @pl.when(c == 0)
    def _():
        reduce_3(3)

    @pl.when(c == 1)
    def _():
        last_3()

    wait(tok.at[pl.ds(0, 127)], s_send.at[0])
    wait(part.at[pl.ds(0, 30)], s_send.at[1])


def shards_fn(tokens, coefficients, gate_weights, up_weights):
    dma = pltpu.SemaphoreType.DMA
    hidden = pl.pallas_call(
        kernel,
        out_shape=jax.ShapeDtypeStruct((2, 4, 16, 256), jnp.bfloat16),
        in_specs=[
            pl.BlockSpec(memory_space=pl.ANY),
            pl.BlockSpec(memory_space=pltpu.SMEM),
            pl.BlockSpec(memory_space=pl.ANY),
            pl.BlockSpec(memory_space=pl.ANY),
        ],
        out_specs=pl.BlockSpec(memory_space=pltpu.VMEM),
        scratch_shapes=[
            pltpu.VMEM((128, 16, 4096), jnp.bfloat16),
            pltpu.VMEM((4096, 512), jnp.bfloat16),
            pltpu.VMEM((32, 4, 16, 512), jnp.float32),
            pltpu.VMEM((16, 4, 16, 512), jnp.float32),
            pltpu.VMEM((4, 4, 4, 16, 512), jnp.float32),
            pltpu.VMEM((4, 4, 4, 16, 512), jnp.float32),
            pltpu.VMEM((4, 3, 2, 16, 512), jnp.float32),
            pltpu.VMEM((3, 4, 16, 512), jnp.float32),
            dma((3,)), dma((2,)), dma((4, 2)), dma((4, 3)), dma((4, 2, 2)), dma((4, 2)),
            dma((4, 2)), dma((4, 2)), dma((4, 4)), dma((4, 3, 2)), dma((3, 4)),
        ],
        compiler_params=pltpu.CompilerParams(collective_id=0, has_side_effects=True, vmem_limit_bytes=60 * 1024 * 1024),
    )(tokens, coefficients, gate_weights, up_weights)
    return hidden.reshape(1, 128, 256)


def solution(mesh):
    return jax.shard_map(
        shards_fn,
        mesh=mesh,
        in_specs=(P("src", "tp", "row"), P(), P("src", "row", "tp"), P("src", "row", "tp")),
        out_specs=P("src", "row", "tp"),
        check_vma=False,
    )
```
